32 devices in a mesh: parts: 2 (over y), space: 4 (over z), filt: 2 (over x), rep: 2 (over core).
Axes of the slice: x: 2, y: 2, z: 4, core: 2. Of those that a mesh axis runs over, the one named last changes fastest.
Arguments:
- features: bfloat16 [128, 512, 256], P(('parts', 'space'), 'filt', 'rep'), parts along dimension 0, may hold values from -6 to 6
- kernel: bfloat16 [3, 3, 512, 512], P(None, None, 'filt'), may hold values from -0.09375 to 0.09375
- shift_bias: float32 [512], P('filt'), may hold values from -3 to 3
- upstream: bfloat16 [128, 512, 256], P(('parts', 'space'), 'filt', 'rep'), parts along dimension 0, may hold values from -6 to 6
Outputs:
- block_out: bfloat16 [128, 512, 256], P(('parts', 'space'), 'filt', 'rep'), parts along dimension 0
- input_grad: bfloat16 [128, 512, 256], P(('parts', 'space'), 'filt', 'rep'), parts along dimension 0
- kernel_grad: float32 [6, 3, 512, 512], P('parts', None, 'filt'), parts along dimension 0
- bias_grad: float32 [1024], P(('parts', 'filt')), parts along dimension 0
The draws below stay inside these ranges and needn't reach their ends.
There are 2 independent parts, one for each index of `parts`. The reference program is written for one: setup_inputs(seed, part) draws one part's arguments, and reference() takes and returns one part's arrays. A program takes and returns all parts, laid end to end along the dimension named above; an argument that names none is the same for every part. Nothing has to cross between parts.
All inputs are finite; a program needn't handle non-finite values.
Results may differ from the reference program's by a relative error of at most 0.0055.
Values may be sent and summed in bfloat16 or wider, within the bound.
No kernel may reach another device: no remote copies, remote signals or barrier semaphores. Data moves between devices by JAX's collectives and lax.ppermute only.
A program may use at most 64 MiB of HBM per device.

```python
import jax
import jax.numpy as jnp
from jax import lax

C = 512
NH = 64
NW = 256


def levels(own_key, extent, split, smallest, high):
    def one(axis_at, blocks):
        steps = jax.random.uniform(jax.random.fold_in(jax.random.fold_in(own_key, 6), axis_at), (blocks,), jnp.float32, smallest / len(split), high / len(split))
        return jnp.repeat(jnp.exp(steps), extent[axis_at] // blocks).reshape((-1,) + (1,) * (len(extent) - axis_at - 1))

    level = one(*split[0])
    for cut in split[1:]:
        level = level * one(*cut)
    return level


def centred(own_key, dims, spread, reach, split=(), dtype=jnp.bfloat16):
    loudness = levels(own_key, dims, split, -0.22, 0.18) if split else 1.0
    values = jax.random.normal(own_key, dims, jnp.float32) * spread * loudness
    return jnp.minimum(jnp.maximum(values, -reach), reach).astype(dtype)


def setup_inputs(seed: int = 0, part: int = 0) -> dict:
    splits = jax.random.split(jax.random.key(seed), 5)
    part_keys = jax.random.split(jax.random.fold_in(splits[4], part), 5)
    return {
        "features": centred(part_keys[0], (NH, C, NW), 1.0, 6.0, ((0, 4), (1, 2), (2, 2))),
        "kernel": centred(splits[1], (3, 3, C, C), (9 * C) ** -0.5, 0.09375, ((2, 2),)),
        "shift_bias": centred(splits[2], (C,), 0.5, 3.0, ((0, 2),), jnp.float32),
        "upstream": centred(part_keys[3], (NH, C, NW), 1.0, 6.0, ((0, 4), (1, 2), (2, 2))),
    }


def reference(features, kernel, shift_bias, upstream):
    feat = jnp.transpose(features, (0, 2, 1))
    upper = jnp.transpose(upstream, (0, 2, 1))
    kern = jnp.transpose(kernel, (0, 1, 3, 2))
    height, width, chans = feat.shape
    padded = jnp.pad(feat, ((1, 1), (1, 1), (0, 0)))
    pre = jnp.zeros((height * width, chans), jnp.float32) + shift_bias[None, :]
    for row_tap in range(3):
        for col_tap in range(3):
            window = padded[row_tap:row_tap + height, col_tap:col_tap + width].reshape(-1, chans)
            pre = pre + jnp.dot(window, kern[row_tap, col_tap], preferred_element_type=jnp.float32)
    pre = pre.reshape(height, width, chans)
    sigm = jax.nn.sigmoid(pre)
    block_out = (feat.astype(jnp.float32) + pre * sigm).astype(jnp.bfloat16)
    slope = (upper.astype(jnp.float32) * sigm * (1.0 + pre * (1.0 - sigm))).astype(jnp.bfloat16)
    slope_pad = jnp.pad(slope, ((1, 1), (1, 1), (0, 0)))
    back = jnp.zeros((height * width, chans), jnp.float32)
    kernel_rows = []
    flat_slope = slope.reshape(-1, chans)
    for row_tap in range(3):
        taps_row = []
        for col_tap in range(3):
            part_slope = slope_pad[2 - row_tap:2 - row_tap + height, 2 - col_tap:2 - col_tap + width].reshape(-1, chans)
            back = back + jnp.dot(part_slope, kern[row_tap, col_tap].T, preferred_element_type=jnp.float32)
            window = padded[row_tap:row_tap + height, col_tap:col_tap + width].reshape(-1, chans)
            taps_row.append(jnp.dot(flat_slope.T, window, preferred_element_type=jnp.float32))
        kernel_rows.append(jnp.stack(taps_row))
    scale = 1.0 / jnp.sqrt(jnp.float32(height * width))
    input_grad = (upper.astype(jnp.float32) + back.reshape(height, width, chans)).astype(jnp.bfloat16)
    kernel_grad = jnp.stack(kernel_rows) * scale
    bias_grad = lax.optimization_barrier(jnp.sum(flat_slope.astype(jnp.float32), axis=0)) * scale
    return (jnp.transpose(block_out, (0, 2, 1)), jnp.transpose(input_grad, (0, 2, 1)), kernel_grad, bias_grad)
```

```python
import jax
import jax.numpy as jnp
from jax import lax
from jax.sharding import PartitionSpec as P

F32 = jnp.float32
BF16 = jnp.bfloat16


def shift_perm(count, step):
    return [(i, (i + step) % count) for i in range(count)]


def row_halos(cells):
    count = lax.axis_size("space")
    ends = count - 1
    upper = lax.ppermute(cells[-1:], "space", [(i, i + 1) for i in range(ends)])
    lower = lax.ppermute(cells[:1], "space", [(i + 1, i) for i in range(ends)])
    return upper, lower


def col_halos(cells):
    count = lax.axis_size("rep")
    spot = lax.axis_index("rep")
    first, last = cells[:, :, 0], cells[:, :, -1]
    if count == 2:
        got = lax.ppermute(jnp.where(spot == 0, last, first), "rep", [(0, 1), (1, 0)])
        none = jnp.zeros_like(got)
        return jnp.where(spot == 0, none, got), jnp.where(spot == 0, got, none)
    ends = count - 1
    left = lax.ppermute(last, "rep", [(i, i + 1) for i in range(ends)])
    right = lax.ppermute(first, "rep", [(i + 1, i) for i in range(ends)])
    return left, right


def spread(cells, left, right):
    before = jnp.concatenate([left[:, :, None], cells[:, :, :-1]], axis=2)
    after = jnp.concatenate([cells[:, :, 1:], right[:, :, None]], axis=2)
    return before, after


def to_middle_and_back(part):
    count = lax.axis_size("space")
    spot = lax.axis_index("space")
    low, high = count // 2 - 1, count // 2
    for step in range(low):
        got = lax.ppermute(part, "space", [(step, step + 1), (count - 1 - step, count - 2 - step)])
        part = (part.astype(F32) + got.astype(F32)).astype(BF16)
    got = lax.ppermute(part, "space", [(low, high), (high, low)])
    part = (part.astype(F32) + got.astype(F32)).astype(BF16)
    for step in reversed(range(low)):
        got = lax.ppermute(part, "space", [(step + 1, step), (count - 2 - step, count - 1 - step)])
        part = jnp.where((spot == step) | (spot == count - 1 - step), got, part)
    return part


def per_device(features, kernel, shift_bias, upstream):
    rows, local, cols = upstream.shape
    groups = lax.axis_size("filt")
    mine = lax.axis_index("filt")
    half = lax.axis_index("rep")
    taken = [lax.rem(mine + step, groups) for step in range(groups)]
    cuts = [0, 5, 10, rows - 1]
    remote = [
        [
            lax.ppermute(features[lo:hi], "filt", shift_perm(groups, -step))
            for lo, hi in zip(cuts[:-1], cuts[1:])
        ]
        for step in range(1, groups)
    ]
    upper, lower = row_halos(features)
    tall = jnp.concatenate([upper, features, lower], axis=0)
    left, right = col_halos(tall)
    rim_rows = jnp.concatenate([features[rows - 1 :], lower, upper], axis=0)
    rim_cols = jnp.concatenate([left, right], axis=0)
    lefts, rights, talls = [left], [right], [tall]
    for step in range(1, groups):
        got_rows = lax.ppermute(rim_rows, "filt", shift_perm(groups, -step))
        got_cols = lax.ppermute(rim_cols, "filt", shift_perm(groups, -step))
        lefts.append(got_cols[: rows + 2])
        rights.append(got_cols[rows + 2 :])
        talls.append((remote[step - 1], got_rows))

    def block(lo, hi):
        out = [[], [], []]
        for step in range(groups):
            if step == 0:
                cells = tall[lo:hi]
            else:
                pieces, rim = talls[step]
                parts = []
                if lo == 0:
                    parts.append(rim[2:3])
                for piece, start, stop in zip(pieces, cuts[:-1], cuts[1:]):
                    low, high = max(lo - 1, start), min(hi - 1, stop)
                    if low < high:
                        parts.append(piece[low - start : high - start])
                if hi >= rows + 1:
                    parts.append(rim[: hi - rows])
                cells = jnp.concatenate(parts, axis=0) if len(parts) > 1 else parts[0]
            before, after = spread(cells, lefts[step][lo:hi], rights[step][lo:hi])
            out[0].append(before)
            out[1].append(cells)
            out[2].append(after)
        return jnp.concatenate(out[0] + out[1] + out[2], axis=1)

    stacked = jnp.concatenate(
        [lax.dynamic_slice_in_dim(kernel, t * local, local, axis=3) for t in taken], axis=3
    )
    depth = 3 * stacked.shape[3]
    forward_w = jnp.transpose(stacked, (0, 2, 1, 3)).reshape(3, local, depth)

    def forward(cells, lo, hi):
        count = hi - lo
        pre = jnp.zeros((count, local, cols), F32) + shift_bias[None, :, None]
        for tap in range(3):
            pre = pre + jnp.einsum(
                "ok,hkj->hoj", forward_w[tap], cells[tap : tap + count], preferred_element_type=F32
            )
        sigm = jax.nn.sigmoid(pre)
        out = (features[lo:hi].astype(F32) + pre * sigm).astype(BF16)
        slope = (upstream[lo:hi].astype(F32) * sigm * (1.0 + pre * (1.0 - sigm))).astype(BF16)
        return out, slope

    def weight_grad(cells, slope):
        count = slope.shape[0]
        return [
            jnp.einsum(
                "hoj,hkj->ok", slope, cells[tap : tap + count], preferred_element_type=F32
            )
            for tap in range(3)
        ]

    spans = [(1, 4), (4, 9), (9, rows - 2), (rows - 2, rows), (0, 1)]
    outs, slopes, sums = {}, {}, None
    for lo, hi in spans:
        cells = block(lo, hi + 2)
        outs[lo], slopes[lo] = forward(cells, lo, hi)
        grads = weight_grad(cells, slopes[lo])
        sums = grads if sums is None else [s + g for s, g in zip(sums, grads)]
    order = sorted(outs)
    block_out = jnp.concatenate([outs[lo] for lo in order], axis=0)
    slope = jnp.concatenate([slopes[lo] for lo in order], axis=0)

    bias_part = jnp.sum(slope.astype(F32), axis=(0, 2))
    sums[0] = jnp.concatenate(
        [sums[0], jnp.broadcast_to(bias_part[:, None], (local, 128))], axis=1
    )
    halves = local // 2
    chunks = []
    for tap in range(3):
        away = lax.dynamic_slice_in_dim(sums[tap], (1 - half) * halves, halves, axis=0)
        keep = lax.dynamic_slice_in_dim(sums[tap], half * halves, halves, axis=0)
        got = lax.ppermute(away.astype(BF16), "rep", [(0, 1), (1, 0)])
        both = (keep + got.astype(F32)).astype(BF16)
        if tap == 2:
            chunks.append(both[: halves // 2])
            chunks.append(both[halves // 2 :])
        else:
            chunks.append(both)
    chunks = [to_middle_and_back(part) for part in chunks]

    s_upper, s_lower = row_halos(slope)
    s_tall = jnp.concatenate([s_upper, slope, s_lower], axis=0)
    s_left, s_right = col_halos(s_tall)
    s_before, s_after = spread(s_tall, s_left, s_right)
    s_all = jnp.concatenate([s_after, s_tall, s_before], axis=1)
    backward_w = jnp.transpose(stacked, (0, 3, 1, 2)).reshape(3, groups * local, 3 * local)

    def backward(step, lo, hi):
        count = hi - lo
        total = jnp.zeros((count, local, cols), F32)
        for tap in range(3):
            total = total + jnp.einsum(
                "ck,hkj->hcj",
                backward_w[tap, step * local : (step + 1) * local],
                s_all[lo + 2 - tap : lo + 2 - tap + count],
                preferred_element_type=F32,
            )
        return total

    pieces = [(0, 4), (4, 8), (8, 12), (12, rows)]
    got = {}
    for lo, hi in pieces:
        for step in range(1, groups):
            away = backward(step, lo, hi).astype(BF16)
            got[lo, step] = lax.ppermute(away, "filt", shift_perm(groups, step))
    grad_in = []
    for lo, hi in pieces:
        total = upstream[lo:hi].astype(F32) + backward(0, lo, hi)
        for step in range(1, groups):
            total = total + got[lo, step].astype(F32)
        grad_in.append(total.astype(BF16))
    input_grad = jnp.concatenate(grad_in, axis=0)

    whole = []
    parts = [chunks[0], chunks[1], jnp.concatenate(chunks[2:], axis=0)]
    total_cells = rows * cols * lax.axis_size("space") * lax.axis_size("rep")
    scale = 1.0 / jnp.sqrt(jnp.float32(total_cells))
    bias_grad = None
    for tap, part in enumerate(parts):
        other = lax.ppermute(part, "rep", [(0, 1), (1, 0)])
        full = jnp.where(
            half == 0,
            jnp.concatenate([part, other], axis=0),
            jnp.concatenate([other, part], axis=0),
        )
        if tap == 0:
            bias_grad = full[:, depth].astype(F32) * scale
            full = full[:, :depth]
        full = full.reshape(local, 3, groups, local)
        pick = full
        for turn in range(1, groups):
            pick = jnp.where(mine == turn, jnp.roll(full, turn, axis=2), pick)
        full = pick.reshape(local, 3, groups * local)
        whole.append(jnp.transpose(full, (1, 0, 2)).astype(F32) * scale)
    return block_out, input_grad, jnp.stack(whole), bias_grad


def solution(mesh):
    in_specs = (
        P(("parts", "space"), "filt", "rep"),
        P(None, None, "filt", None),
        P("filt"),
        P(("parts", "space"), "filt", "rep"),
    )
    out_specs = (
        P(("parts", "space"), "filt", "rep"),
        P(("parts", "space"), "filt", "rep"),
        P("parts", None, "filt", None),
        P(("parts", "filt")),
    )
    return jax.shard_map(
        per_device, mesh=mesh, in_specs=in_specs, out_specs=out_specs, check_vma=False
    )
```

```python
import functools

import jax
import jax.numpy as jnp
from jax import lax
from jax.experimental import pallas as pl
from jax.experimental.pallas import tpu as pltpu
from jax.sharding import PartitionSpec as P

F32 = jnp.float32
BF16 = jnp.bfloat16
LANES = 128
VMEM_BYTES = 40 * 2**20


def shift_perm(count, step):
    return [(i, (i + step) % count) for i in range(count)]


def swap_rep(cells):
    return lax.ppermute(cells, "rep", [(0, 1), (1, 0)])


def send_rows(cells, edge):
    count = lax.axis_size("space")
    down = jnp.concatenate([cells[-1:], edge[None]], axis=0)
    up = jnp.concatenate([cells[:1], edge[None]], axis=0)
    return down, up, [(i, i + 1) for i in range(count - 1)], [(i + 1, i) for i in range(count - 1)]


def edge_kernel(cells, out):
    core = lax.axis_index("rep")
    rows = cells.shape[0]
    lane = lax.broadcasted_iota(jnp.int32, out.shape, 1)
    total = jnp.zeros(out.shape, F32)
    for row in range(rows):
        value = cells[row].astype(F32)
        moved = pltpu.roll(value, row + 2, 1)
        plain = pltpu.roll(value, row + 1, 1)
        total = jnp.where(lane == row + 1, jnp.where(core == 0, moved, plain), total)
    out[...] = total.astype(BF16)


def column_shifts(value, edge, p, core, lane):
    wide = value.astype(F32)
    border = pltpu.roll(edge, LANES - 1 - p + core, 1)
    before = pltpu.roll(wide, 1, 1)
    after = pltpu.roll(wide, LANES - 1, 1)
    none = jnp.zeros_like(border)
    before = jnp.where(lane == 0, jnp.where(core == 1, border, none), before)
    after = jnp.where(lane == LANES - 1, jnp.where(core == 0, border, none), after)
    return before.astype(BF16), after.astype(BF16)


def forward_kernel(runs, rows, cuts, groups, has_sum, last, names, *refs):
    ref = dict(zip(names, refs))
    cells_x, slope_x = ref["cells"], ref["slope_all"]
    core = lax.axis_index("rep")
    mine = lax.axis_index("filt")
    local = ref["features"].shape[1]
    step = pl.program_id(0)

    @pl.when(step == 0)
    def _():
        lane = lax.broadcasted_iota(jnp.int32, (local, LANES), 1)
        for turn in range(groups):
            def source(row):
                if turn == 0:
                    if row < 0:
                        return ref["above"][0], ref["above"][1], rows
                    if row >= rows:
                        return ref["below"][0], ref["below"][1], 1
                    return ref["features"][row], ref["edge"][...], row + 1
                a, b, c, d = [f"{part}{turn}" for part in "abcd"]
                if row < 0:
                    return ref[d][2], ref[d][4], rows
                if row >= rows:
                    return ref[d][1], ref[d][3], 1
                edge = ref[b][cuts[1] - cuts[0]]
                if row < cuts[0]:
                    return ref[a][row], edge, row + 1
                if row < cuts[1]:
                    return ref[b][row - cuts[0]], edge, row + 1
                if row < cuts[2]:
                    return ref[c][row - cuts[1]], edge, row + 1
                return ref[d][0], edge, row + 1

            base = pl.multiple_of(lax.rem(mine + turn, groups) * local, local)
            block = 0
            for start, count in runs:
                for row in range(start - 1, start + count + 1):
                    value, edge, p = source(row)
                    before, after = column_shifts(value, edge.astype(F32), p, core, lane)
                    where = (pl.ds(base, local), pl.ds(block * LANES, LANES))
                    cells_x[(0,) + where] = before
                    cells_x[(1,) + where] = value
                    cells_x[(2,) + where] = after
                    block += 1
        edges = jnp.zeros((local, LANES), F32)
        block, place = 0, 0
        for start, count in runs:
            total = None
            for row_tap in range(3):
                for col_tap in range(3):
                    window = cells_x[
                        col_tap, :, (block + row_tap) * LANES : (block + row_tap + count) * LANES
                    ]
                    term = jnp.dot(
                        ref["kernel"][row_tap, col_tap], window, preferred_element_type=F32
                    )
                    total = term if total is None else total + term
            for at in range(count):
                row = start + at
                pre = total[:, at * LANES : (at + 1) * LANES] + ref["bias"][...]
                sigm = jax.nn.sigmoid(pre)
                out = ref["features"][row].astype(F32) + pre * sigm
                ref["block_out"][place] = out.astype(BF16)
                slope = ref["upstream"][row].astype(F32) * sigm * (1.0 + pre * (1.0 - sigm))
                slope = slope.astype(BF16)
                ref["slope"][place] = slope
                slope_x[:, place * LANES : (place + 1) * LANES] = slope
                wide = slope.astype(F32)
                moved = pltpu.roll(wide, row + 2, 1)
                plain = pltpu.roll(wide, row + 1, 1)
                edges = jnp.where(lane == row + 1, jnp.where(core == 0, moved, plain), edges)
                place += 1
            block += count + 2
        if "edge_in" in ref:
            edges = edges + ref["edge_in"][...].astype(F32)
        ref["edge_out"][...] = edges.astype(BF16)

    def grads(row_tap, col_tap):
        block, place, total = 0, 0, None
        for start, count in runs:
            window = cells_x[
                col_tap, :, pl.ds(pl.multiple_of((block + row_tap) * LANES, LANES), count * LANES)
            ]
            term = lax.dot_general(
                slope_x[:, place * LANES : (place + count) * LANES],
                window,
                (((1,), (1,)), ((), ())),
                preferred_element_type=F32,
            )
            total = term if total is None else total + term
            block += count + 2
            place += count
        return total

    width = slope_x.shape[1]
    bias = lax.dot_general(
        jnp.ones((16, width), BF16), slope_x[...], (((1,), (1,)), ((), ())),
        preferred_element_type=F32,
    )
    if "bias_in" in ref:
        bias = bias + ref["bias_in"][...]
    if not last:
        ref["bias_out"][...] = bias
        for col_tap in range(3):
            total = grads(step, col_tap)
            if has_sum:
                total = total + ref["sum_in"][0, col_tap]
            ref["sum_out"][0, col_tap] = total
        return
    halves = local // 2
    own = pl.multiple_of(core * halves, halves)
    other = pl.multiple_of((1 - core) * halves, halves)
    hold = ref["hold"]
    for tap in range(3):
        @pl.when(step == tap)
        def _():
            for col_tap in range(3):
                hold[...] = grads(tap, col_tap) + ref["sum_in"][0, col_tap]
                at = col_tap * halves
                ref[f"away{tap}"][at : at + halves] = hold[pl.ds(other, halves)].astype(BF16)
                ref[f"keep{tap}"][at : at + halves] = hold[pl.ds(own, halves)]
            if tap == 0:
                at = 3 * halves
                ref["away0"][at:] = jnp.zeros((16, hold.shape[1]), BF16)
                ref["keep0"][at:] = jnp.zeros((16, hold.shape[1]), F32)
                ref["away0"][at:, :local] = bias.astype(BF16)
                ref["keep0"][at:, :local] = bias


def backward_kernel(rows_out, parts, rows, turn, groups, names, *refs):
    ref = dict(zip(names, refs))
    cells_x = ref["cells"]
    core = lax.axis_index("rep")
    local = cells_x.shape[1]
    lane = lax.broadcasted_iota(jnp.int32, (local, LANES), 1)

    def source(row):
        if row < 0:
            return ref["above"][0], ref["above"][1], rows
        if row >= rows:
            return ref["below"][0], ref["below"][1], 1
        for at, held in enumerate(parts):
            if row in held:
                return ref[f"slope{at}"][held.index(row)], ref["edge"][...], row + 1

    target = lax.rem(lax.axis_index("filt") + turn, groups)
    channels = pl.ds(pl.multiple_of(target * local, local), local)
    block, place = 0, 0
    for start, count in rows_out:
        for at, row in enumerate(range(start - 1, start + count + 1)):
            value, edge, p = source(row)
            before, after = column_shifts(value, edge.astype(F32), p, core, lane)
            lanes = pl.ds((block + at) * LANES, LANES)
            cells_x[0, :, lanes] = after
            cells_x[1, :, lanes] = value
            cells_x[2, :, lanes] = before
        total = None
        for row_tap in range(3):
            for col_tap in range(3):
                first = block + 2 - row_tap
                term = jnp.dot(
                    ref["weights"][row_tap, col_tap, channels],
                    cells_x[col_tap, :, first * LANES : (first + count) * LANES],
                    preferred_element_type=F32,
                )
                total = term if total is None else total + term
        for at in range(count):
            piece = total[:, at * LANES : (at + 1) * LANES]
            if "upstream" in ref:
                piece = piece + ref["upstream"][start + at].astype(F32)
            ref["out"][place] = piece.astype(ref["out"].dtype)
            place += 1
        block += count + 2


def finish_kernel(taps, scale, names, *refs):
    ref = dict(zip(names, refs))
    core = lax.axis_index("rep")
    halves = ref["out"].shape[2] // 2
    own = pl.multiple_of(core * halves, halves)
    other = pl.multiple_of((1 - core) * halves, halves)
    for tap in taps:
        @pl.when(pl.program_id(0) == tap - taps[0])
        def _():
            for col_tap in range(3):
                for who, where in (("mine", own), ("other", other)):
                    at = col_tap * halves
                    if tap == 2:
                        low = ref[f"{who}2"].shape[0]
                        for lo in range(0, halves, 16):
                            pos = at + lo
                            name, pos = (f"{who}2", pos) if pos < low else (f"{who}3", pos - low)
                            ref["out"][0, col_tap, pl.ds(pl.multiple_of(where + lo, 16), 16)] = (
                                ref[name][pos : pos + 16].astype(F32) * scale
                            )
                    else:
                        ref["out"][0, col_tap, pl.ds(where, halves)] = (
                            ref[f"{who}{tap}"][at : at + halves].astype(F32) * scale
                        )
    if "bias" in ref:
        local = ref["bias"].shape[1]
        ref["bias"][...] = ref["mine0"][3 * halves :, :local].astype(F32) * scale


def params(bytes_limit=VMEM_BYTES):
    return pltpu.CompilerParams(vmem_limit_bytes=bytes_limit)


def whole_spec(array):
    zeros = (0,) * array.ndim
    return pl.BlockSpec(array.shape, lambda *_: zeros)


def call(body, inputs, outputs, scratch, grid=(1,), specs=None, out_specs=None, aliases=None, flops=0):
    names = list(inputs) + list(outputs) + list(scratch)
    specs, out_specs = specs or {}, out_specs or {}
    shapes = {key: jax.ShapeDtypeStruct(*value) for key, value in outputs.items()}
    got = pl.pallas_call(
        functools.partial(body, names),
        grid=grid,
        in_specs=[specs.get(key) or whole_spec(value) for key, value in inputs.items()],
        out_specs=[out_specs.get(key) or whole_spec(value) for key, value in shapes.items()],
        out_shape=list(shapes.values()),
        scratch_shapes=[pltpu.VMEM(*value) for value in scratch.values()],
        input_output_aliases=aliases or {},
        compiler_params=params(),
        cost_estimate=pl.CostEstimate(flops=flops, bytes_accessed=4 * 2**20, transcendentals=0),
    )(*inputs.values())
    return dict(zip(shapes, got))


def per_device(features, kernel, shift_bias, upstream):
    rows, local, cols = upstream.shape
    groups = lax.axis_size("filt")
    chans = kernel.shape[3]
    halves = local // 2
    turns = range(1, groups)
    third = (rows - 1) // 3
    cuts = (third, 2 * third, rows - 1)

    def gather(cells):
        return {t: lax.ppermute(cells, "filt", shift_perm(groups, -t)) for t in turns}

    got = {"a": gather(features[: cuts[0]])}
    edge = call(
        lambda names, *refs: edge_kernel(*refs),
        {"cells": features},
        {"edge": ((local, LANES), BF16)},
        {},
    )["edge"]
    edge = swap_rep(edge)
    got["b"] = gather(jnp.concatenate([features[cuts[0] : cuts[1]], edge[None]], axis=0))
    down, up, down_perm, up_perm = send_rows(features, edge)
    above = lax.ppermute(down, "space", down_perm)
    below = lax.ppermute(up, "space", up_perm)
    got["c"] = gather(features[cuts[1] : cuts[2]])
    rim = jnp.concatenate(
        [features[cuts[2] :], below[:1], above[:1], below[1:], above[1:]], axis=0
    )
    got["d"] = gather(rim)
    weights_t = jnp.swapaxes(kernel, 2, 3)
    bias_wide = jnp.broadcast_to(shift_bias[:, None], (local, LANES))

    sets = [
        ("ab", [(1, cuts[1] - 2)]),
        ("bc", [(cuts[1] - 1, rows - 1 - cuts[1])]),
        ("abcd", [(rows - 2, 2), (0, 1)]),
    ]
    outs, slopes, held = [], [], []
    carried = {}
    for at, (parts, runs) in enumerate(sets):
        last = at == 2
        count = sum(n for _, n in runs)
        blocks = sum(n + 2 for _, n in runs)
        inputs = {
            "kernel": kernel,
            "bias": bias_wide,
            "features": features,
            "upstream": upstream,
            "edge": edge,
        }
        if last:
            inputs["above"], inputs["below"] = above, below
        for part in parts:
            for t in turns:
                inputs[f"{part}{t}"] = got[part][t]
        inputs.update(carried)
        specs = {"sum_in": pl.BlockSpec((1, 3, local, chans), lambda i: (i, 0, 0, 0))}
        outputs = {
            "block_out": ((count, local, cols), BF16),
            "slope": ((count, local, cols), BF16),
            "edge_out": ((local, LANES), BF16),
        }
        scratch = {
            "cells": ((3, chans, blocks * LANES), BF16),
            "slope_all": ((local, count * LANES), BF16),
        }
        aliases = {}
        if last:
            for tap in range(3):
                height = 3 * halves + (16 if tap == 0 else 0)
                outputs[f"away{tap}"] = ((height, chans), BF16)
                outputs[f"keep{tap}"] = ((height, chans), F32)
            scratch["hold"] = ((local, chans), F32)
        else:
            outputs["bias_out"] = ((16, local), F32)
            outputs["sum_out"] = ((3, 3, local, chans), F32)
            if at:
                aliases = {list(inputs).index("sum_in"): list(outputs).index("sum_out")}
        done = call(
            functools.partial(forward_kernel, runs, rows, cuts, groups, at > 0, last),
            inputs,
            outputs,
            scratch,
            grid=(3,),
            specs=specs,
            out_specs={"sum_out": pl.BlockSpec((1, 3, local, chans), lambda i: (i, 0, 0, 0))},
            aliases=aliases,
            flops=36 * local * chans * count * cols,
        )
        outs.append(done["block_out"])
        slopes.append(done["slope"])
        held.append([s + i for s, n in runs for i in range(n)])
        if not last:
            carried = {
                "edge_in": done["edge_out"],
                "bias_in": done["bias_out"],
                "sum_in": done["sum_out"],
            }
    block_out = jnp.concatenate([outs[2][2:], outs[0], outs[1], outs[2][:2]], axis=0)

    space = lax.axis_size("space")
    spot = lax.axis_index("space")
    low, high = space // 2 - 1, space // 2
    chunks = []
    for tap in range(3):
        came = swap_rep(done[f"away{tap}"])
        both = (done[f"keep{tap}"] + came.astype(F32)).astype(BF16)
        if tap == 2:
            cut = both.shape[0] // 2
            chunks += [both[:cut], both[cut:]]
        else:
            chunks.append(both)
    finals, others = [], []
    for part in chunks:
        for step in range(low):
            came = lax.ppermute(
                part, "space", [(step, step + 1), (space - 1 - step, space - 2 - step)]
            )
            part = (part.astype(F32) + came.astype(F32)).astype(BF16)
        came = lax.ppermute(part, "space", [(low, high), (high, low)])
        part = (part.astype(F32) + came.astype(F32)).astype(BF16)
        for step in reversed(range(low)):
            came = lax.ppermute(
                part, "space", [(step + 1, step), (space - 2 - step, space - 1 - step)]
            )
            part = jnp.where((spot == step) | (spot == space - 1 - step), came, part)
        finals.append(part)
        others.append(swap_rep(part))

    s_edge = swap_rep(done["edge_out"])
    s_first, s_last = slopes[2][2:], slopes[2][1:2]
    s_down = jnp.concatenate([s_last, s_edge[None]], axis=0)
    s_up = jnp.concatenate([s_first, s_edge[None]], axis=0)
    s_above = lax.ppermute(s_down, "space", down_perm)
    s_below = lax.ppermute(s_up, "space", up_perm)

    def backward(turn, runs, dtype):
        count = sum(n for _, n in runs)
        blocks = sum(n + 2 for _, n in runs)
        inputs = {"weights": weights_t, "edge": s_edge}
        for at, piece in enumerate(slopes):
            inputs[f"slope{at}"] = piece
        if any(s == 0 or s + n == rows for s, n in runs):
            inputs["above"], inputs["below"] = s_above, s_below
        if turn == 0:
            inputs["upstream"] = upstream
        return call(
            functools.partial(backward_kernel, runs, held, rows, turn, groups),
            inputs,
            {"out": ((count, local, cols), dtype)},
            {"cells": ((3, local, blocks * LANES), BF16)},
            flops=18 * local * local * count * cols,
        )["out"]

    mid = rows // 2
    pieces = [[(1, mid - 1)], [(mid, rows - 1 - mid)], [(0, 1), (rows - 1, 1)]]
    came = []
    for runs in pieces:
        arrived = []
        for t in turns:
            away = backward(t, runs, BF16)
            arrived.append(lax.ppermute(away, "filt", shift_perm(groups, t)))
        came.append(arrived)
    own = backward(0, [(0, rows)], F32)
    total = own
    for at in range(groups - 1):
        ends = came[2][at]
        whole = jnp.concatenate([ends[:1], came[0][at], came[1][at], ends[1:]], axis=0)
        total = total + whole.astype(F32)
    input_grad = total.astype(BF16)

    total_cells = rows * cols * space * lax.axis_size("rep")
    scale = 1.0 / float(total_cells) ** 0.5
    inputs = {"mine0": finals[0], "other0": others[0], "mine1": finals[1], "other1": others[1]}
    out_shape = ((3, 3, local, chans), F32)
    first = call(
        functools.partial(finish_kernel, (0, 1), scale),
        inputs,
        {"out": out_shape, "bias": ((16, local), F32)},
        {},
        grid=(2,),
        out_specs={"out": pl.BlockSpec((1, 3, local, chans), lambda i: (i, 0, 0, 0))},
    )
    inputs = {
        "mine2": finals[2], "mine3": finals[3], "other2": others[2], "other3": others[3],
        "before": first["out"],
    }
    kernel_grad = call(
        functools.partial(finish_kernel, (2,), scale),
        inputs,
        {"out": out_shape},
        {},
        specs={"before": pl.BlockSpec(memory_space=pl.ANY)},
        out_specs={"out": pl.BlockSpec((1, 3, local, chans), lambda i: (2, 0, 0, 0))},
        aliases={4: 0},
    )["out"]
    return block_out, input_grad, kernel_grad, first["bias"][0]


def solution(mesh):
    in_specs = (
        P(("parts", "space"), "filt", "rep"),
        P(None, None, "filt", None),
        P("filt"),
        P(("parts", "space"), "filt", "rep"),
    )
    out_specs = (
        P(("parts", "space"), "filt", "rep"),
        P(("parts", "space"), "filt", "rep"),
        P("parts", None, "filt", None),
        P(("parts", "filt")),
    )

    return jax.shard_map(
        per_device, mesh=mesh, in_specs=in_specs, out_specs=out_specs, check_vma=False
    )
```
